32 devices in a mesh: seq: 8 (over y, x, core), head: 4 (over z).
Axes of the slice: x: 2, y: 2, z: 4, core: 2. Of those that a mesh axis runs over, the one named last changes fastest.
Arguments:
- lengths: int32 [16], replicated, may hold values from 1 to 1024, 2048 in all
- query: bfloat16 [2048, 8192], P('seq', 'head'), may hold values from -4.5 to 4.5
- keys: bfloat16 [2048, 1024], P('seq', 'head'), may hold values from -4.5 to 4.5
- values: bfloat16 [2048, 1024], P('seq', 'head'), may hold values from -6 to 6
- attention_grad: bfloat16 [2048, 8192], P('seq', 'head'), may hold values from -6 to 6
Outputs:
- attention_out: bfloat16 [2048, 8192], P('seq', 'head')
- query_grad: bfloat16 [2048, 8192], P('seq', 'head')
- key_grad: bfloat16 [2048, 1024], P('seq', 'head')
- value_grad: bfloat16 [2048, 1024], P('seq', 'head')
The draws below stay inside these ranges and needn't reach their ends.
Inputs may be any that keep to these rules, and one draw needn't show every extreme that they name: The lengths sum to 2048 and the longest is exactly 1024.
All inputs are finite; a program needn't handle non-finite values.
Results may differ from the reference program's by a relative error of at most 0.023.
Values may be sent and summed in bfloat16 or wider, within the bound.
A program may use at most 128 MiB of HBM per device.

```python
import math
import jax
import jax.numpy as jnp
import numpy as np
from jax import lax

ATT_HEADS = 64
KV_HEADS = 8
ATT_DIM = 128
DOCS = 16
PACKED_TOKENS = 2048
DOC_MOST = 1024


def query_key_pair(key):
    width_query = ATT_HEADS * ATT_DIM
    width_key = KV_HEADS * ATT_DIM
    query = jnp.clip(jax.random.normal(jax.random.fold_in(key, 11), (PACKED_TOKENS, width_query)), -4.0, 4.0)
    keyed = jnp.clip(jax.random.normal(jax.random.fold_in(key, 12), (PACKED_TOKENS, width_key)), -4.0, 4.0)
    return (query, keyed)


def draw_query(key, part):
    return query_key_pair(key)[0].astype(jnp.bfloat16)


def draw_keys(key, part):
    return query_key_pair(key)[1].astype(jnp.bfloat16)


def levels(own_key, shape, pieces, low, top_value):
    def one(axis_at, parts):
        steps = jax.random.uniform(jax.random.fold_in(jax.random.fold_in(own_key, 6), axis_at), (parts,), jnp.float32, low / len(pieces), top_value / len(pieces))
        return jnp.repeat(jnp.exp(steps), shape[axis_at] // parts).reshape((-1,) + (1,) * (len(shape) - axis_at - 1))

    level = one(*pieces[0])
    for cut in pieces[1:]:
        level = level * one(*cut)
    return level


def profile(count, total, most, skew):
    loads = [(1 << 20) // math.isqrt(rank ** skew) + 1 for rank in range(2, count + 1)]
    surplus, holding = total - most - (count - 1), [1] * (count - 1)
    while surplus > 0:
        candidates = [i for i in range(count - 1) if holding[i] < most]
        whole, left = sum([loads[i] for i in candidates]), surplus
        for i in candidates:
            more = min(most - holding[i], max(1, left * loads[i] // whole), surplus)
            holding[i] = holding[i] + more
            surplus = surplus - more
    return np.array([most] + holding)


def uneven(own_key, amount, total, most, lean):
    if amount == 2:
        one = jax.random.randint(own_key, (), max(1, total - most), min(most, total - 1) + 1)
        return jnp.stack([one, total - one])
    sizes = jnp.asarray(profile(amount, total, most, lean), jnp.int32)
    pairs = (amount - 1) // 2
    donor, sink = sizes[1:1 + 2 * pairs:2], sizes[2:2 + 2 * pairs:2]
    margin = jnp.minimum(donor - 1, most - sink)
    passed = jax.random.randint(jax.random.fold_in(own_key, 1), (pairs,), 0, 1 << 20) % (margin + 1)
    sizes = sizes.at[1:1 + 2 * pairs:2].set(donor - passed).at[2:2 + 2 * pairs:2].set(sink + passed)
    return sizes[jax.random.permutation(jax.random.fold_in(own_key, 2), amount)]


def bell_draw(stream_key, dims, deviation, most, cuts=(), kind=jnp.bfloat16):
    entries = jax.random.normal(stream_key, dims, jnp.float32) * deviation
    if len(cuts) > 0:
        entries = levels(stream_key, dims, cuts, -0.22, 0.18) * entries
    return jnp.clip(entries, min=-most, max=most).astype(kind)


def setup_inputs(seed: int = 0) -> dict:
    seeds = jax.random.split(jax.random.key(seed), 6)
    lengths = uneven(seeds[0], DOCS, PACKED_TOKENS, DOC_MOST, 2).astype(jnp.int32)
    query = draw_query(jax.random.fold_in(seeds[5], 71), 0)
    keys = draw_keys(jax.random.fold_in(seeds[5], 71), 0)
    values = bell_draw(seeds[3], (PACKED_TOKENS, KV_HEADS * ATT_DIM), 1.0, 6.0, ((0, 8), (1, 4)))
    attention_grad = bell_draw(seeds[4], (PACKED_TOKENS, ATT_HEADS * ATT_DIM), 1.0, 6.0, ((0, 8), (1, 4)))
    return {"lengths": lengths, "query": query, "keys": keys, "values": values, "attention_grad": attention_grad}


masked_score = -1.0e30


def segment_of(position, ends):
    return jnp.sum((ends[None, :] <= position[:, None]).astype(jnp.int32), axis=1)


def reference(lengths, query, keys, values, attention_grad):
    total = query.shape[0]
    share = ATT_HEADS // KV_HEADS
    position = jnp.arange(total, dtype=jnp.int32)
    ends = jnp.cumsum(lengths).astype(jnp.int32)
    segment = segment_of(position, ends)
    allowed = (segment[:, None] == segment[None, :]) & (position[:, None] >= position[None, :])
    scale = ATT_DIM ** -0.5
    group_of = jnp.arange(ATT_HEADS, dtype=jnp.int32) // share

    def split_heads(array, count):
        return array.reshape(total, count, ATT_DIM).transpose(1, 0, 2)

    def one_head(operands):
        head_q, head_k, head_v, head_g = operands
        score = jnp.dot(head_q, head_k.T, preferred_element_type=jnp.float32) * scale
        score = jnp.where(allowed, score, masked_score)
        top = jnp.max(score, axis=1, keepdims=True)
        mass = jnp.sum(jnp.where(allowed, jnp.exp(score - top), 0.0), axis=1, keepdims=True)
        log_total = top + jnp.log(mass)
        prob = jnp.where(allowed, jnp.exp(score - log_total), 0.0)
        prob_b = prob.astype(jnp.bfloat16)
        attn_out = jnp.dot(prob_b, head_v, preferred_element_type=jnp.float32)
        delta = jnp.sum(head_g.astype(jnp.float32) * attn_out, axis=1, keepdims=True)
        dprob = jnp.dot(head_g, head_v.T, preferred_element_type=jnp.float32)
        dscore = (prob * (dprob - delta) * scale).astype(jnp.bfloat16)
        grad_q = jnp.dot(dscore, head_k, preferred_element_type=jnp.float32).astype(jnp.bfloat16)
        grad_k = jnp.dot(dscore.T, head_q, preferred_element_type=jnp.float32)
        grad_v = jnp.dot(prob_b.T, head_g, preferred_element_type=jnp.float32)
        return attn_out.astype(jnp.bfloat16), grad_q, grad_k, grad_v

    key_heads = split_heads(keys, KV_HEADS)[group_of]
    value_heads = split_heads(values, KV_HEADS)[group_of]
    outputs, grad_q, grad_k, grad_v = lax.map(one_head, (split_heads(query, ATT_HEADS), key_heads, value_heads, split_heads(attention_grad, ATT_HEADS)))
    grad_k = jnp.sum(grad_k.reshape(KV_HEADS, share, total, ATT_DIM), axis=1).astype(jnp.bfloat16)
    grad_v = jnp.sum(grad_v.reshape(KV_HEADS, share, total, ATT_DIM), axis=1).astype(jnp.bfloat16)

    def merge_heads(array):
        return array.transpose(1, 0, 2).reshape(total, -1)

    return (merge_heads(outputs), merge_heads(grad_q), merge_heads(grad_k), merge_heads(grad_v))
```

```python
import functools

import jax
import jax.numpy as jnp
from jax import lax
from jax.experimental import pallas as pl
from jax.experimental.pallas import tpu as pltpu
from jax.sharding import PartitionSpec as P

ATT_DIM = 128
LOG2E = 1.4426950408889634
MASKED = -1.0e30
MESH = pl.DeviceIdType.MESH

F32 = jnp.float32
BF16 = jnp.bfloat16
NT = (((1,), (1,)), ((), ()))
NN = (((1,), (0,)), ((), ()))


def kernel(
    n, span, kv_count, share,
    lengths, query, keys, values, grad,
    out, query_grad, key_grad, value_grad,
    kv, key_t, value_t, score, prob, dscore, acc, own, sent, got,
    gather_send, gather_recv, back_send, back_recv,
):
    rows = query.shape[0]
    scale = ATT_DIM ** -0.5
    me = lax.axis_index("seq")

    barrier = pltpu.get_barrier_semaphore()
    for k in range(1, span):
        @pl.when(me + k < n)
        def _():
            pl.semaphore_signal(barrier, inc=1, device_id={"seq": me + k}, device_id_type=MESH)

        @pl.when(me - k >= 0)
        def _():
            pl.semaphore_signal(barrier, inc=1, device_id={"seq": me - k}, device_id_type=MESH)

    def stage(g, _):
        columns = pl.ds(pl.multiple_of(g * ATT_DIM, ATT_DIM), ATT_DIM)
        kv[g, 0, 0] = keys[:, columns]
        kv[g, 0, 1] = values[:, columns]
        for k in range(1, span):
            @pl.when(me - k < 0)
            def _():
                kv[g, k] = jnp.zeros((2, rows, ATT_DIM), BF16)
        return 0

    lax.fori_loop(0, kv_count, stage, 0)
    pl.semaphore_wait(
        barrier, jnp.minimum(me, span - 1) + jnp.minimum(n - 1 - me, span - 1)
    )

    def gather(g, k):
        return pltpu.make_async_remote_copy(
            src_ref=kv.at[g, 0],
            dst_ref=kv.at[g, k],
            send_sem=gather_send.at[g, k],
            recv_sem=gather_recv.at[g, k],
            device_id={"seq": me + k},
            device_id_type=MESH,
        )

    def back(g, k):
        return pltpu.make_async_remote_copy(
            src_ref=sent.at[g, k],
            dst_ref=got.at[g, k],
            send_sem=back_send.at[g, k],
            recv_sem=back_recv.at[g, k],
            device_id={"seq": me - k},
            device_id_type=MESH,
        )

    def send_all(g, _):
        for k in range(1, span):
            @pl.when(me + k < n)
            def _():
                gather(g, k).start()
        return 0

    lax.fori_loop(0, kv_count, send_all, 0)

    q_lane = lax.broadcasted_iota(jnp.int32, (1, rows), 1)
    position = q_lane + me * rows
    start = jnp.zeros((1, rows), jnp.int32)
    end = 0
    for i in range(lengths.shape[0]):
        end = end + lengths[i]
        start = jnp.where(position >= end, end, start)

    def group(g, _):
        for k in range(1, span):
            @pl.when(me - k >= 0)
            def _():
                gather(g, k).wait_recv()
        for k in range(span):
            key_t[:, k * rows:(k + 1) * rows] = kv[g, k, 0].T
            value_t[:, k * rows:(k + 1) * rows] = kv[g, k, 1].T
        acc[...] = jnp.zeros_like(acc)

        def head(i, _):
            columns = pl.ds(pl.multiple_of((g * share + i) * ATT_DIM, ATT_DIM), ATT_DIM)
            q = query[:, columns]
            top = jnp.full((1, rows), MASKED, F32)
            k_row = lax.broadcasted_iota(jnp.int32, (rows, rows), 0)
            for k in range(span):
                s = lax.dot_general(kv[g, k, 0], q, NT, preferred_element_type=F32)
                allow = k_row >= start - (me - k) * rows
                if k == 0:
                    allow = allow & (k_row <= q_lane)
                s = jnp.where(allow, s, MASKED)
                score[k * rows:(k + 1) * rows, :] = s
                top = jnp.maximum(top, jnp.max(s, axis=0, keepdims=True))
            mass = jnp.zeros((1, rows), F32)
            for k in range(span):
                at = slice(k * rows, (k + 1) * rows)
                p = jnp.exp2((score[at, :] - top) * (scale * LOG2E))
                mass = mass + jnp.sum(p, axis=0, keepdims=True)
                score[at, :] = p
                prob[at, :] = p.astype(BF16)
            inverse = 1.0 / mass
            out_t = lax.dot_general(value_t[...], prob[...], NN, preferred_element_type=F32)
            out_t = out_t * inverse
            out[:, columns] = out_t.T.astype(BF16)
            grad_t = grad[:, columns].astype(F32).T
            factor = inverse * scale
            delta = jnp.sum(grad_t * out_t, axis=0, keepdims=True) * factor
            grad_t = grad_t * factor
            grad_s = grad_t.T.astype(BF16)
            grad_t = grad_t.astype(BF16)
            for k in range(span):
                at = slice(k * rows, (k + 1) * rows)
                dp = lax.dot_general(kv[g, k, 1], grad_t, NN, preferred_element_type=F32)
                dscore[at, :] = (score[at, :] * (dp - delta)).astype(BF16)
            acc[1] += lax.dot_general(prob[...], grad_s, NN, preferred_element_type=F32)
            acc[0] += lax.dot_general(dscore[...], q, NN, preferred_element_type=F32)
            dq = lax.dot_general(key_t[...], dscore[...], NN, preferred_element_type=F32)
            query_grad[:, columns] = dq.T.astype(BF16)
            return 0

        lax.fori_loop(0, share, head, 0)
        for k in range(1, span):
            @pl.when(me - k >= 0)
            def _():
                sent[g, k, 0] = acc[0, k * rows:(k + 1) * rows, :].astype(BF16)
                sent[g, k, 1] = (acc[1, k * rows:(k + 1) * rows, :] * (1.0 / scale)).astype(BF16)
                back(g, k).start()
        own[g, 0] = acc[0, 0:rows, :]
        own[g, 1] = acc[1, 0:rows, :] * (1.0 / scale)
        return 0

    lax.fori_loop(0, kv_count, group, 0)

    def finish(g, _):
        columns = pl.ds(pl.multiple_of(g * ATT_DIM, ATT_DIM), ATT_DIM)
        for k in range(1, span):
            @pl.when(me + k < n)
            def _():
                back(g, k).wait_recv()
                own[g] = own[g] + got[g, k].astype(F32)
        key_grad[:, columns] = own[g, 0].astype(BF16)
        value_grad[:, columns] = own[g, 1].astype(BF16)
        for k in range(1, span):
            @pl.when(me + k < n)
            def _():
                gather(g, k).wait_send()

            @pl.when(me - k >= 0)
            def _():
                back(g, k).wait_send()
        return 0

    lax.fori_loop(0, kv_count, finish, 0)


def on_device(lengths, query, keys, values, attention_grad):
    n = lax.axis_size("seq")
    rows = query.shape[0]
    kv_count = keys.shape[1] // ATT_DIM
    share = query.shape[1] // keys.shape[1]
    span = n // 2 + 1
    whole = pl.BlockSpec(memory_space=pltpu.VMEM)
    return pl.pallas_call(
        functools.partial(kernel, n, span, kv_count, share),
        out_shape=[
            jax.ShapeDtypeStruct(a.shape, BF16) for a in (query, query, keys, values)
        ],
        in_specs=[pl.BlockSpec(memory_space=pltpu.SMEM)] + [whole] * 4,
        out_specs=[whole] * 4,
        scratch_shapes=[
            pltpu.VMEM((kv_count, span, 2, rows, ATT_DIM), BF16),
            pltpu.VMEM((ATT_DIM, span * rows), BF16),
            pltpu.VMEM((ATT_DIM, span * rows), BF16),
            pltpu.VMEM((span * rows, rows), F32),
            pltpu.VMEM((span * rows, rows), BF16),
            pltpu.VMEM((span * rows, rows), BF16),
            pltpu.VMEM((2, span * rows, ATT_DIM), F32),
            pltpu.VMEM((kv_count, 2, rows, ATT_DIM), F32),
            pltpu.VMEM((kv_count, span, 2, rows, ATT_DIM), BF16),
            pltpu.VMEM((kv_count, span, 2, rows, ATT_DIM), BF16),
            pltpu.SemaphoreType.DMA((kv_count, span)),
            pltpu.SemaphoreType.DMA((kv_count, span)),
            pltpu.SemaphoreType.DMA((kv_count, span)),
            pltpu.SemaphoreType.DMA((kv_count, span)),
        ],
        compiler_params=pltpu.CompilerParams(
            collective_id=0, has_side_effects=True, vmem_limit_bytes=48 << 20
        ),
    )(lengths, query, keys, values, attention_grad)


def solution(mesh):
    in_specs = (P(), P("seq", "head"), P("seq", "head"), P("seq", "head"), P("seq", "head"))
    out_specs = (P("seq", "head"), P("seq", "head"), P("seq", "head"), P("seq", "head"))
    return jax.shard_map(
        on_device, mesh=mesh, in_specs=in_specs, out_specs=out_specs, check_vma=False
    )
```

```python
import functools

import jax
import jax.numpy as jnp
from jax import lax
from jax.experimental import pallas as pl
from jax.experimental.pallas import tpu as pltpu
from jax.sharding import PartitionSpec as P

ATT_DIM = 128
LOG2E = 1.4426950408889634
MASKED = -1.0e30
MESH = pl.DeviceIdType.MESH

F32 = jnp.float32
BF16 = jnp.bfloat16
NT = (((1,), (1,)), ((), ()))
NN = (((1,), (0,)), ((), ()))


def kernel(
    n, span, kv_count, share, lead,
    lengths, query_hbm, keys, values, grad_hbm,
    out, query_grad, key_grad, value_grad,
    query, grad, kv, key_t, value_t, score, prob, dscore, acc, sent, mix, got,
    load, gather_send, gather_recv, back_send, mix_recv, back_recv,
):
    rows = query.shape[0]
    scale = ATT_DIM ** -0.5
    me = lax.axis_index("seq")
    odd = lax.rem(me, 2)
    pair = me + 1 - 2 * odd
    far = span // 2

    def load_kv(g, which):
        columns = pl.ds(pl.multiple_of(g * ATT_DIM, ATT_DIM), ATT_DIM)
        source = (keys, values)[which]
        return pltpu.make_async_copy(
            source.at[:, columns], kv.at[g, 0, which], load.at[2 + 2 * g + which]
        )

    def start_load(g, _):
        load_kv(g, 0).start()
        load_kv(g, 1).start()
        return 0

    lax.fori_loop(0, kv_count, start_load, 0)
    load_query = pltpu.make_async_copy(query_hbm, query, load.at[0])
    load_grad = pltpu.make_async_copy(grad_hbm, grad, load.at[1])
    load_query.start()
    load_grad.start()

    def signal(barrier, target):
        pl.semaphore_signal(barrier, inc=1, device_id={"seq": target}, device_id_type=MESH)

    barrier = pltpu.get_barrier_semaphore()
    signal(barrier, pair)
    for j in range(1, far + 1):
        @pl.when(me + 2 * j < n)
        def _():
            signal(barrier, me + 2 * j)

        @pl.when(me - 2 * j >= 0)
        def _():
            signal(barrier, me - 2 * j)

    def clear(g, _):
        for k in range(1, span):
            @pl.when(me - k < 0)
            def _():
                kv[g, k] = jnp.zeros((2, rows, ATT_DIM), BF16)
        return 0

    lax.fori_loop(0, kv_count, clear, 0)
    pl.semaphore_wait(
        barrier, 1 + jnp.minimum(me // 2, far) + jnp.minimum((n - 1 - me) // 2, far)
    )

    def remote(source, target, send_sem, recv_sem, device):
        return pltpu.make_async_remote_copy(
            src_ref=source, dst_ref=target, send_sem=send_sem, recv_sem=recv_sem,
            device_id={"seq": device}, device_id_type=MESH,
        )

    def gather(g, j):
        return remote(
            kv.at[g, 0], kv.at[g, 2 * j], gather_send.at[g, 2 * j],
            gather_recv.at[g, 2 * j], me + 2 * j,
        )

    def hand_on(g, j, slot):
        return remote(
            kv.at[g, 2 * j], kv.at[g, slot], gather_send.at[g, slot],
            gather_recv.at[g, slot], pair,
        )

    def each_hand_on(first, last, act):
        for j in range(first, last + 1):
            if j >= 1:
                @pl.when((odd == 1) & (me - 2 * j >= 0))
                def _():
                    act(j, 2 * j - 1)
            if j < far:
                @pl.when((odd == 0) & (me - 2 * j >= 0))
                def _():
                    act(j, 2 * j + 1)

    def begin(g, _):
        load_kv(g, 0).wait()
        load_kv(g, 1).wait()
        for j in range(1, far + 1):
            @pl.when(me + 2 * j < n)
            def _():
                gather(g, j).start()
        each_hand_on(0, 0, lambda j, slot: hand_on(g, j, slot).start())
        return 0

    lax.fori_loop(0, kv_count, begin, 0)

    def pass_on(g):
        for j in range(1, far + 1):
            @pl.when(me - 2 * j >= 0)
            def _():
                gather(g, j).wait_recv()
            each_hand_on(j, j, lambda j, slot: hand_on(g, j, slot).start())

    def partial(g, k):
        at = slice(k * rows, (k + 1) * rows)
        return acc[g, 0, at, :], acc[g, 1, at, :] * (1.0 / scale)

    def to_pair(g, k, j):
        return remote(
            sent.at[g, k], mix.at[g, j], back_send.at[g, k], mix_recv.at[g, j], pair
        )

    def back(g, j):
        return remote(
            sent.at[g, 2 * j], got.at[g, j], back_send.at[g, 2 * j],
            back_recv.at[g, j], me - 2 * j,
        )

    def each_to_pair(act):
        for k in range(1, span, 2):
            @pl.when((odd == 1) & (me - k >= 0))
            def _():
                act(k, (k - 1) // 2)

            @pl.when((odd == 0) & (me - k >= 0))
            def _():
                act(k, (k + 1) // 2)

    def share_partial(g):
        def act(k, j):
            dk, dv = partial(g, k)
            sent[g, k, 0] = dk.astype(BF16)
            sent[g, k, 1] = dv.astype(BF16)
            to_pair(g, k, j).start()

        each_to_pair(act)

    def wait_mix(g, j):
        to_pair(g, 1, j).wait_recv()

    def combine(g):
        for j in range(far, 0, -1):
            def relay(mixed):
                dk, dv = partial(g, 2 * j)
                if mixed:
                    wait_mix(g, j)
                    dk = dk + mix[g, j, 0].astype(F32)
                    dv = dv + mix[g, j, 1].astype(F32)
                sent[g, 2 * j, 0] = dk.astype(BF16)
                sent[g, 2 * j, 1] = dv.astype(BF16)
                back(g, j).start()

            if j < far:
                @pl.when(me - 2 * j >= 0)
                def _():
                    relay(True)
            else:
                @pl.when((me - 2 * j >= 0) & (odd == 1))
                def _():
                    relay(True)

                @pl.when((me - 2 * j >= 0) & (odd == 0))
                def _():
                    relay(False)

    q_lane = lax.broadcasted_iota(jnp.int32, (1, rows), 1)
    position = q_lane + me * rows
    start = jnp.zeros((1, rows), jnp.int32)
    end = 0
    for i in range(lengths.shape[0]):
        end = end + lengths[i]
        start = jnp.where(position >= end, end, start)

    load_query.wait()
    load_grad.wait()
    pass_on(0)
    steps = share // lead

    def group(g, _):
        for k in range(1, span, 2):
            @pl.when(me - k >= 0)
            def _():
                hand_on(g, 0, k).wait_recv()
        for k in range(span):
            key_t[:, k * rows:(k + 1) * rows] = kv[g, k, 0].T
            value_t[:, k * rows:(k + 1) * rows] = kv[g, k, 1].T
        acc[g] = jnp.zeros(acc.shape[1:], F32)

        def one(i, slot):
            sc, pr, ds = score.at[slot], prob.at[slot], dscore.at[slot]
            columns = pl.ds(pl.multiple_of((g * share + i) * ATT_DIM, ATT_DIM), ATT_DIM)
            q = query[:, columns]
            top = jnp.full((1, rows), MASKED, F32)
            k_row = lax.broadcasted_iota(jnp.int32, (rows, rows), 0)
            for k in range(span):
                s = lax.dot_general(kv[g, k, 0], q, NT, preferred_element_type=F32)
                allow = k_row >= start - (me - k) * rows
                if k == 0:
                    allow = allow & (k_row <= q_lane)
                s = jnp.where(allow, s, MASKED)
                sc[k * rows:(k + 1) * rows, :] = s
                top = jnp.maximum(top, jnp.max(s, axis=0, keepdims=True))
            yield
            mass = jnp.zeros((1, rows), F32)
            for k in range(span):
                at = slice(k * rows, (k + 1) * rows)
                p = jnp.exp2((sc[at, :] - top) * (scale * LOG2E))
                mass = mass + jnp.sum(p, axis=0, keepdims=True)
                sc[at, :] = p
                pr[at, :] = p.astype(BF16)
            inverse = 1.0 / mass
            out_t = lax.dot_general(value_t[...], pr[...], NN, preferred_element_type=F32)
            out_t = out_t * inverse
            out[:, columns] = out_t.T.astype(BF16)
            grad_t = grad[:, columns].astype(F32).T
            factor = inverse * scale
            delta = jnp.sum(grad_t * out_t, axis=0, keepdims=True) * factor
            grad_t = grad_t * factor
            grad_s = grad_t.T.astype(BF16)
            grad_t = grad_t.astype(BF16)
            yield
            for k in range(span):
                at = slice(k * rows, (k + 1) * rows)
                dp = lax.dot_general(kv[g, k, 1], grad_t, NN, preferred_element_type=F32)
                ds[at, :] = (sc[at, :] * (dp - delta)).astype(BF16)
            acc[g, 1] += lax.dot_general(pr[...], grad_s, NN, preferred_element_type=F32)
            yield
            acc[g, 0] += lax.dot_general(ds[...], q, NN, preferred_element_type=F32)
            dq = lax.dot_general(key_t[...], ds[...], NN, preferred_element_type=F32)
            query_grad[:, columns] = dq.T.astype(BF16)
            yield

        def head(i, _):
            if kv_count > 1:
                @pl.when((i == min(1, steps - 1)) & (g >= 1))
                def _():
                    combine(g - 1)

                @pl.when((i == steps // 2) & (g + 1 < kv_count))
                def _():
                    pass_on(g + 1)
            runs = [one(lead * i + slot, slot) for slot in range(lead)]
            for _ in range(4):
                for run in runs:
                    next(run)
            return 0

        lax.fori_loop(0, steps, head, 0)
        share_partial(g)
        return 0

    lax.fori_loop(0, kv_count, group, 0)
    combine(kv_count - 1)

    def finish(g, _):
        columns = pl.ds(pl.multiple_of(g * ATT_DIM, ATT_DIM), ATT_DIM)

        @pl.when(odd == 0)
        def _():
            wait_mix(g, 0)
            acc[g, 0, 0:rows, :] += mix[g, 0, 0].astype(F32)
            acc[g, 1, 0:rows, :] += mix[g, 0, 1].astype(F32) * scale

        for j in range(1, far + 1):
            @pl.when(me + 2 * j < n)
            def _():
                back(g, j).wait_recv()
                acc[g, 0, 0:rows, :] += got[g, j, 0].astype(F32)
                acc[g, 1, 0:rows, :] += got[g, j, 1].astype(F32) * scale
        dk, dv = partial(g, 0)
        key_grad[:, columns] = dk.astype(BF16)
        value_grad[:, columns] = dv.astype(BF16)
        for j in range(1, far + 1):
            @pl.when(me + 2 * j < n)
            def _():
                gather(g, j).wait_send()

            @pl.when(me - 2 * j >= 0)
            def _():
                back(g, j).wait_send()
        each_hand_on(0, far, lambda j, slot: hand_on(g, j, slot).wait_send())
        each_to_pair(lambda k, j: to_pair(g, k, j).wait_send())
        return 0

    lax.fori_loop(0, kv_count, finish, 0)


def on_device(lengths, query, keys, values, attention_grad):
    n = lax.axis_size("seq")
    rows = query.shape[0]
    kv_count = keys.shape[1] // ATT_DIM
    share = query.shape[1] // keys.shape[1]
    span = n // 2 + 1
    lead = 2
    whole = pl.BlockSpec(memory_space=pltpu.VMEM)
    block = (2, rows, ATT_DIM)
    return pl.pallas_call(
        functools.partial(kernel, n, span, kv_count, share, lead),
        out_shape=[
            jax.ShapeDtypeStruct(a.shape, BF16) for a in (query, query, keys, values)
        ],
        in_specs=[pl.BlockSpec(memory_space=pltpu.SMEM)]
        + [pl.BlockSpec(memory_space=pl.ANY)] * 4,
        out_specs=[whole] * 4,
        scratch_shapes=[
            pltpu.VMEM(query.shape, BF16),
            pltpu.VMEM(query.shape, BF16),
            pltpu.VMEM((kv_count, span) + block, BF16),
            pltpu.VMEM((ATT_DIM, span * rows), BF16),
            pltpu.VMEM((ATT_DIM, span * rows), BF16),
            pltpu.VMEM((lead, span * rows, rows), F32),
            pltpu.VMEM((lead, span * rows, rows), BF16),
            pltpu.VMEM((lead, span * rows, rows), BF16),
            pltpu.VMEM((kv_count, 2, span * rows, ATT_DIM), F32),
            pltpu.VMEM((kv_count, span) + block, BF16),
            pltpu.VMEM((kv_count, span // 2 + 1) + block, BF16),
            pltpu.VMEM((kv_count, span // 2 + 1) + block, BF16),
            pltpu.SemaphoreType.DMA((2 + 2 * kv_count,)),
            pltpu.SemaphoreType.DMA((kv_count, span)),
            pltpu.SemaphoreType.DMA((kv_count, span)),
            pltpu.SemaphoreType.DMA((kv_count, span)),
            pltpu.SemaphoreType.DMA((kv_count, span // 2 + 1)),
            pltpu.SemaphoreType.DMA((kv_count, span // 2 + 1)),
        ],
        compiler_params=pltpu.CompilerParams(
            collective_id=0, has_side_effects=True, vmem_limit_bytes=60 << 20
        ),
    )(lengths, query, keys, values, attention_grad)


def solution(mesh):
    in_specs = (P(), P("seq", "head"), P("seq", "head"), P("seq", "head"), P("seq", "head"))
    out_specs = (P("seq", "head"), P("seq", "head"), P("seq", "head"), P("seq", "head"))
    return jax.shard_map(
        on_device, mesh=mesh, in_specs=in_specs, out_specs=out_specs, check_vma=False
    )
```

```python
import functools

import jax
import jax.numpy as jnp
from jax import lax
from jax.experimental import pallas as pl
from jax.experimental.pallas import tpu as pltpu
from jax.sharding import PartitionSpec as P

ATT_DIM = 128
LOG2E = 1.4426950408889634
MASKED = -1.0e30
MESH = pl.DeviceIdType.MESH

F32 = jnp.float32
BF16 = jnp.bfloat16
NT = (((1,), (1,)), ((), ()))
NN = (((1,), (0,)), ((), ()))


def kernel(
    n, span, kv_count, share, lead,
    lengths, query_hbm, keys, values, grad_hbm,
    out, query_grad, key_grad, value_grad,
    query, grad, kv, key_t, value_t, score, prob, dscore, acc, sent, mix, got,
    load, gather_send, gather_recv, back_send, mix_recv, back_recv,
):
    rows = query.shape[0]
    scale = ATT_DIM ** -0.5
    me = lax.axis_index("seq")
    odd = lax.rem(me, 2)
    pair = me + 1 - 2 * odd
    far = span // 2

    def load_kv(g, which):
        columns = pl.ds(pl.multiple_of(g * ATT_DIM, ATT_DIM), ATT_DIM)
        source = (keys, values)[which]
        return pltpu.make_async_copy(
            source.at[:, columns], kv.at[g, 0, which], load.at[2 + 2 * g + which]
        )

    def start_load(g, _):
        load_kv(g, 0).start()
        load_kv(g, 1).start()
        return 0

    lax.fori_loop(0, kv_count, start_load, 0)
    load_query = pltpu.make_async_copy(query_hbm, query, load.at[0])
    load_grad = pltpu.make_async_copy(grad_hbm, grad, load.at[1])
    load_query.start()
    load_grad.start()

    def signal(barrier, target):
        pl.semaphore_signal(barrier, inc=1, device_id={"seq": target}, device_id_type=MESH)

    barrier = pltpu.get_barrier_semaphore()
    signal(barrier, pair)
    for j in range(1, far + 1):
        @pl.when(me + 2 * j < n)
        def _():
            signal(barrier, me + 2 * j)

        @pl.when(me - 2 * j >= 0)
        def _():
            signal(barrier, me - 2 * j)

    def clear(g, _):
        for k in range(1, span):
            @pl.when(me - k < 0)
            def _():
                kv[g, k] = jnp.zeros((2, rows, ATT_DIM), BF16)
        return 0

    lax.fori_loop(0, kv_count, clear, 0)
    pl.semaphore_wait(
        barrier, 1 + jnp.minimum(me // 2, far) + jnp.minimum((n - 1 - me) // 2, far)
    )

    def remote(source, target, send_sem, recv_sem, device):
        return pltpu.make_async_remote_copy(
            src_ref=source, dst_ref=target, send_sem=send_sem, recv_sem=recv_sem,
            device_id={"seq": device}, device_id_type=MESH,
        )

    def gather(g, j):
        return remote(
            kv.at[g, 0], kv.at[g, 2 * j], gather_send.at[g, 2 * j],
            gather_recv.at[g, 2 * j], me + 2 * j,
        )

    def hand_on(g, j, slot):
        return remote(
            kv.at[g, 2 * j], kv.at[g, slot], gather_send.at[g, slot],
            gather_recv.at[g, slot], pair,
        )

    def each_hand_on(first, last, act):
        for j in range(first, last + 1):
            if j >= 1:
                @pl.when((odd == 1) & (me - 2 * j >= 0))
                def _():
                    act(j, 2 * j - 1)
            if j < far:
                @pl.when((odd == 0) & (me - 2 * j >= 0))
                def _():
                    act(j, 2 * j + 1)

    def begin(g):
        load_kv(g, 0).wait()
        load_kv(g, 1).wait()
        for j in range(1, far + 1):
            @pl.when(me + 2 * j < n)
            def _():
                gather(g, j).start()
        each_hand_on(0, 0, lambda j, slot: hand_on(g, j, slot).start())

    begin(0)

    def pass_on(g):
        for j in range(1, far + 1):
            @pl.when(me - 2 * j >= 0)
            def _():
                gather(g, j).wait_recv()
            each_hand_on(j, j, lambda j, slot: hand_on(g, j, slot).start())

    def partial(g, k):
        at = slice(k * rows, (k + 1) * rows)
        return acc[g, 0, at, :], acc[g, 1, at, :] * (1.0 / scale)

    def to_pair(g, k, j):
        return remote(
            sent.at[g, k], mix.at[g, j], back_send.at[g, k], mix_recv.at[g, j], pair
        )

    def back(g, j):
        return remote(
            sent.at[g, 2 * j], got.at[g, j], back_send.at[g, 2 * j],
            back_recv.at[g, j], me - 2 * j,
        )

    def each_to_pair(act):
        for k in range(1, span, 2):
            @pl.when((odd == 1) & (me - k >= 0))
            def _():
                act(k, (k - 1) // 2)

            @pl.when((odd == 0) & (me - k >= 0))
            def _():
                act(k, (k + 1) // 2)

    def share_partial(g):
        def act(k, j):
            dk, dv = partial(g, k)
            sent[g, k, 0] = dk.astype(BF16)
            sent[g, k, 1] = dv.astype(BF16)
            to_pair(g, k, j).start()

        each_to_pair(act)

    def wait_mix(g, j):
        to_pair(g, 1, j).wait_recv()

    def combine(g):
        for j in range(far, 0, -1):
            def relay(mixed):
                dk, dv = partial(g, 2 * j)
                if mixed:
                    wait_mix(g, j)
                    dk = dk + mix[g, j, 0].astype(F32)
                    dv = dv + mix[g, j, 1].astype(F32)
                sent[g, 2 * j, 0] = dk.astype(BF16)
                sent[g, 2 * j, 1] = dv.astype(BF16)
                back(g, j).start()

            if j < far:
                @pl.when(me - 2 * j >= 0)
                def _():
                    relay(True)
            else:
                @pl.when((me - 2 * j >= 0) & (odd == 1))
                def _():
                    relay(True)

                @pl.when((me - 2 * j >= 0) & (odd == 0))
                def _():
                    relay(False)

    q_lane = lax.broadcasted_iota(jnp.int32, (1, rows), 1)
    position = q_lane + me * rows
    start = jnp.zeros((1, rows), jnp.int32)
    end = 0
    for i in range(lengths.shape[0]):
        end = end + lengths[i]
        start = jnp.where(position >= end, end, start)

    load_query.wait()
    load_grad.wait()
    pass_on(0)
    steps = share // lead

    def group(g, _):
        for k in range(1, span, 2):
            @pl.when(me - k >= 0)
            def _():
                hand_on(g, 0, k).wait_recv()
        for k in range(span):
            key_t[:, k * rows:(k + 1) * rows] = kv[g, k, 0].T
            value_t[:, k * rows:(k + 1) * rows] = kv[g, k, 1].T
        acc[g] = jnp.zeros(acc.shape[1:], F32)
        if kv_count > 1:
            @pl.when(g + 1 < kv_count)
            def _():
                begin(g + 1)

        def one(i, slot):
            sc, pr, ds = score.at[slot], prob.at[slot], dscore.at[slot]
            columns = pl.ds(pl.multiple_of((g * share + i) * ATT_DIM, ATT_DIM), ATT_DIM)
            q = query[:, columns]
            top = jnp.full((1, rows), MASKED, F32)
            k_row = lax.broadcasted_iota(jnp.int32, (rows, rows), 0)
            for k in range(span):
                s = lax.dot_general(kv[g, k, 0], q, NT, preferred_element_type=F32)
                allow = k_row >= start - (me - k) * rows
                if k == 0:
                    allow = allow & (k_row <= q_lane)
                s = jnp.where(allow, s, MASKED)
                sc[k * rows:(k + 1) * rows, :] = s
                top = jnp.maximum(top, jnp.max(s, axis=0, keepdims=True))
            yield
            mass = jnp.zeros((1, rows), F32)
            for k in range(span):
                at = slice(k * rows, (k + 1) * rows)
                p = jnp.exp2((sc[at, :] - top) * (scale * LOG2E))
                mass = mass + jnp.sum(p, axis=0, keepdims=True)
                sc[at, :] = p
                pr[at, :] = p.astype(BF16)
            inverse = 1.0 / mass
            out_t = lax.dot_general(value_t[...], pr[...], NN, preferred_element_type=F32)
            out_t = out_t * inverse
            out[:, columns] = out_t.T.astype(BF16)
            grad_t = grad[:, columns].astype(F32).T
            factor = inverse * scale
            delta = jnp.sum(grad_t * out_t, axis=0, keepdims=True) * factor
            grad_t = grad_t * factor
            grad_s = grad_t.T.astype(BF16)
            grad_t = grad_t.astype(BF16)
            yield
            for k in range(span):
                at = slice(k * rows, (k + 1) * rows)
                dp = lax.dot_general(kv[g, k, 1], grad_t, NN, preferred_element_type=F32)
                ds[at, :] = (sc[at, :] * (dp - delta)).astype(BF16)
            acc[g, 1] += lax.dot_general(pr[...], grad_s, NN, preferred_element_type=F32)
            yield
            acc[g, 0] += lax.dot_general(ds[...], q, NN, preferred_element_type=F32)
            dq = lax.dot_general(key_t[...], ds[...], NN, preferred_element_type=F32)
            query_grad[:, columns] = dq.T.astype(BF16)
            yield

        def head(i, _):
            if kv_count > 1:
                @pl.when((i == min(1, steps - 1)) & (g >= 1))
                def _():
                    combine(g - 1)

                @pl.when((i == steps - 1) & (g + 1 < kv_count))
                def _():
                    pass_on(g + 1)
            runs = [one(lead * i + slot, slot) for slot in range(lead)]
            for _ in range(4):
                for run in runs:
                    next(run)
            return 0

        lax.fori_loop(0, steps, head, 0)
        share_partial(g)
        return 0

    lax.fori_loop(0, kv_count, group, 0)
    combine(kv_count - 1)

    def finish(g, _):
        columns = pl.ds(pl.multiple_of(g * ATT_DIM, ATT_DIM), ATT_DIM)

        @pl.when(odd == 0)
        def _():
            wait_mix(g, 0)
            acc[g, 0, 0:rows, :] += mix[g, 0, 0].astype(F32)
            acc[g, 1, 0:rows, :] += mix[g, 0, 1].astype(F32) * scale

        for j in range(1, far + 1):
            @pl.when(me + 2 * j < n)
            def _():
                back(g, j).wait_recv()
                acc[g, 0, 0:rows, :] += got[g, j, 0].astype(F32)
                acc[g, 1, 0:rows, :] += got[g, j, 1].astype(F32) * scale
        dk, dv = partial(g, 0)
        key_grad[:, columns] = dk.astype(BF16)
        value_grad[:, columns] = dv.astype(BF16)
        for j in range(1, far + 1):
            @pl.when(me + 2 * j < n)
            def _():
                gather(g, j).wait_send()

            @pl.when(me - 2 * j >= 0)
            def _():
                back(g, j).wait_send()
        each_hand_on(0, far, lambda j, slot: hand_on(g, j, slot).wait_send())
        each_to_pair(lambda k, j: to_pair(g, k, j).wait_send())
        return 0

    lax.fori_loop(0, kv_count, finish, 0)


def on_device(lengths, query, keys, values, attention_grad):
    n = lax.axis_size("seq")
    rows = query.shape[0]
    kv_count = keys.shape[1] // ATT_DIM
    share = query.shape[1] // keys.shape[1]
    span = n // 2 + 1
    lead = 2
    whole = pl.BlockSpec(memory_space=pltpu.VMEM)
    block = (2, rows, ATT_DIM)
    return pl.pallas_call(
        functools.partial(kernel, n, span, kv_count, share, lead),
        out_shape=[
            jax.ShapeDtypeStruct(a.shape, BF16) for a in (query, query, keys, values)
        ],
        in_specs=[pl.BlockSpec(memory_space=pltpu.SMEM)]
        + [pl.BlockSpec(memory_space=pl.ANY)] * 4,
        out_specs=[whole] * 4,
        scratch_shapes=[
            pltpu.VMEM(query.shape, BF16),
            pltpu.VMEM(query.shape, BF16),
            pltpu.VMEM((kv_count, span) + block, BF16),
            pltpu.VMEM((ATT_DIM, span * rows), BF16),
            pltpu.VMEM((ATT_DIM, span * rows), BF16),
            pltpu.VMEM((lead, span * rows, rows), F32),
            pltpu.VMEM((lead, span * rows, rows), BF16),
            pltpu.VMEM((lead, span * rows, rows), BF16),
            pltpu.VMEM((kv_count, 2, span * rows, ATT_DIM), F32),
            pltpu.VMEM((kv_count, span) + block, BF16),
            pltpu.VMEM((kv_count, span // 2 + 1) + block, BF16),
            pltpu.VMEM((kv_count, span // 2 + 1) + block, BF16),
            pltpu.SemaphoreType.DMA((2 + 2 * kv_count,)),
            pltpu.SemaphoreType.DMA((kv_count, span)),
            pltpu.SemaphoreType.DMA((kv_count, span)),
            pltpu.SemaphoreType.DMA((kv_count, span)),
            pltpu.SemaphoreType.DMA((kv_count, span // 2 + 1)),
            pltpu.SemaphoreType.DMA((kv_count, span // 2 + 1)),
        ],
        compiler_params=pltpu.CompilerParams(
            collective_id=0, has_side_effects=True, vmem_limit_bytes=60 << 20
        ),
    )(lengths, query, keys, values, attention_grad)


def solution(mesh):
    in_specs = (P(), P("seq", "head"), P("seq", "head"), P("seq", "head"), P("seq", "head"))
    out_specs = (P("seq", "head"), P("seq", "head"), P("seq", "head"), P("seq", "head"))
    return jax.shard_map(
        on_device, mesh=mesh, in_specs=in_specs, out_specs=out_specs, check_vma=False
    )
```

```python
import functools

import jax
import jax.numpy as jnp
from jax import lax
from jax.experimental import pallas as pl
from jax.experimental.pallas import tpu as pltpu
from jax.sharding import PartitionSpec as P

ATT_DIM = 128
LOG2E = 1.4426950408889634
MASKED = -1.0e30
MESH = pl.DeviceIdType.MESH

F32 = jnp.float32
BF16 = jnp.bfloat16
NT = (((1,), (1,)), ((), ()))
NN = (((1,), (0,)), ((), ()))


def kernel(
    n, span, kv_count, share, lead,
    lengths, query_hbm, keys, values, grad_hbm,
    out, query_grad, key_grad, value_grad,
    query, grad, kv, key_t, value_t, score, prob, dscore, acc, sent, mix, got,
    load, gather_send, gather_recv, back_send, mix_recv, back_recv,
):
    rows = query.shape[0]
    scale = ATT_DIM ** -0.5
    me = lax.axis_index("seq")
    odd = lax.rem(me, 2)
    pair = me + 1 - 2 * odd
    far = span // 2

    def load_kv(g, which):
        columns = pl.ds(pl.multiple_of(g * ATT_DIM, ATT_DIM), ATT_DIM)
        source = (keys, values)[which]
        return pltpu.make_async_copy(
            source.at[:, columns], kv.at[g, 0, which], load.at[2 + 2 * g + which]
        )

    def start_load(g, _):
        load_kv(g, 0).start()
        load_kv(g, 1).start()
        return 0

    lax.fori_loop(0, kv_count, start_load, 0)
    load_query = pltpu.make_async_copy(query_hbm, query, load.at[0])
    load_grad = pltpu.make_async_copy(grad_hbm, grad, load.at[1])
    load_query.start()
    load_grad.start()

    def signal(barrier, target):
        pl.semaphore_signal(barrier, inc=1, device_id={"seq": target}, device_id_type=MESH)

    barrier = pltpu.get_barrier_semaphore()
    signal(barrier, pair)
    for j in range(1, far + 1):
        @pl.when(me + 2 * j < n)
        def _():
            signal(barrier, me + 2 * j)

        @pl.when(me - 2 * j >= 0)
        def _():
            signal(barrier, me - 2 * j)

    def clear(g, _):
        for k in range(1, span):
            @pl.when(me - k < 0)
            def _():
                kv[g, k] = jnp.zeros((2, rows, ATT_DIM), BF16)
        return 0

    lax.fori_loop(0, kv_count, clear, 0)
    pl.semaphore_wait(
        barrier, 1 + jnp.minimum(me // 2, far) + jnp.minimum((n - 1 - me) // 2, far)
    )

    def remote(source, target, send_sem, recv_sem, device):
        return pltpu.make_async_remote_copy(
            src_ref=source, dst_ref=target, send_sem=send_sem, recv_sem=recv_sem,
            device_id={"seq": device}, device_id_type=MESH,
        )

    def gather(g, j):
        return remote(
            kv.at[g, 0], kv.at[g, 2 * j], gather_send.at[g, 2 * j],
            gather_recv.at[g, 2 * j], me + 2 * j,
        )

    def hand_on(g, j, slot):
        return remote(
            kv.at[g, 2 * j], kv.at[g, slot], gather_send.at[g, slot],
            gather_recv.at[g, slot], pair,
        )

    def each_hand_on(first, last, act):
        for j in range(first, last + 1):
            if j >= 1:
                @pl.when((odd == 1) & (me - 2 * j >= 0))
                def _():
                    act(j, 2 * j - 1)
            if j < far:
                @pl.when((odd == 0) & (me - 2 * j >= 0))
                def _():
                    act(j, 2 * j + 1)

    def begin(g):
        load_kv(g, 0).wait()
        load_kv(g, 1).wait()
        for j in range(1, far + 1):
            @pl.when(me + 2 * j < n)
            def _():
                gather(g, j).start()
        each_hand_on(0, 0, lambda j, slot: hand_on(g, j, slot).start())

    begin(0)

    def pass_on(g):
        for j in range(1, far + 1):
            @pl.when(me - 2 * j >= 0)
            def _():
                gather(g, j).wait_recv()
            each_hand_on(j, j, lambda j, slot: hand_on(g, j, slot).start())

    def partial(g, k):
        at = slice(k * rows, (k + 1) * rows)
        return acc[g, 0, at, :], acc[g, 1, at, :] * (1.0 / scale)

    def to_pair(g, k, j):
        return remote(
            sent.at[g, k], mix.at[g, j], back_send.at[g, k], mix_recv.at[g, j], pair
        )

    def back(g, j):
        return remote(
            sent.at[g, 2 * j], got.at[g, j], back_send.at[g, 2 * j],
            back_recv.at[g, j], me - 2 * j,
        )

    def each_to_pair(act):
        for k in range(1, span, 2):
            @pl.when((odd == 1) & (me - k >= 0))
            def _():
                act(k, (k - 1) // 2)

            @pl.when((odd == 0) & (me - k >= 0))
            def _():
                act(k, (k + 1) // 2)

    def share_partial(g):
        def act(k, j):
            dk, dv = partial(g, k)
            sent[g, k, 0] = dk.astype(BF16)
            sent[g, k, 1] = dv.astype(BF16)
            to_pair(g, k, j).start()

        each_to_pair(act)

    def wait_mix(g, j):
        to_pair(g, 1, j).wait_recv()

    def combine(g):
        for j in range(far, 0, -1):
            def relay(mixed):
                dk, dv = partial(g, 2 * j)
                if mixed:
                    wait_mix(g, j)
                    dk = dk + mix[g, j, 0].astype(F32)
                    dv = dv + mix[g, j, 1].astype(F32)
                sent[g, 2 * j, 0] = dk.astype(BF16)
                sent[g, 2 * j, 1] = dv.astype(BF16)
                back(g, j).start()

            if j < far:
                @pl.when(me - 2 * j >= 0)
                def _():
                    relay(True)
            else:
                @pl.when((me - 2 * j >= 0) & (odd == 1))
                def _():
                    relay(True)

                @pl.when((me - 2 * j >= 0) & (odd == 0))
                def _():
                    relay(False)

    q_lane = lax.broadcasted_iota(jnp.int32, (1, rows), 1)
    position = q_lane + me * rows
    start = jnp.zeros((1, rows), jnp.int32)
    end = 0
    for i in range(lengths.shape[0]):
        end = end + lengths[i]
        start = jnp.where(position >= end, end, start)

    load_query.wait()
    load_grad.wait()
    pass_on(0)
    steps = share // lead

    def group(g, _):
        for k in range(1, span, 2):
            @pl.when(me - k >= 0)
            def _():
                hand_on(g, 0, k).wait_recv()
        for k in range(span):
            key_t[:, k * rows:(k + 1) * rows] = kv[g, k, 0].T
            value_t[:, k * rows:(k + 1) * rows] = kv[g, k, 1].T
        acc[g] = jnp.zeros(acc.shape[1:], F32)
        if kv_count > 1:
            @pl.when(g + 1 < kv_count)
            def _():
                begin(g + 1)

        def one(i, slot):
            sc, pr, ds = score.at[slot], prob.at[slot], dscore.at[slot]
            columns = pl.ds(pl.multiple_of((g * share + i) * ATT_DIM, ATT_DIM), ATT_DIM)
            q = query[:, columns]
            top = jnp.full((1, rows), MASKED, F32)
            k_row = lax.broadcasted_iota(jnp.int32, (rows, rows), 0)
            for k in range(span):
                s = lax.dot_general(kv[g, k, 0], q, NT, preferred_element_type=F32)
                allow = k_row >= start - (me - k) * rows
                if k == 0:
                    allow = allow & (k_row <= q_lane)
                s = jnp.where(allow, s, MASKED)
                sc[k * rows:(k + 1) * rows, :] = s
                top = jnp.maximum(top, jnp.max(s, axis=0, keepdims=True))
            yield
            mass = jnp.zeros((1, rows), F32)
            for k in range(span):
                at = slice(k * rows, (k + 1) * rows)
                p = jnp.exp2((sc[at, :] - top) * (scale * LOG2E))
                mass = mass + jnp.sum(p, axis=0, keepdims=True)
                sc[at, :] = p
                pr[at, :] = p.astype(BF16)
            inverse = 1.0 / mass
            out_t = lax.dot_general(value_t[...], pr[...], NN, preferred_element_type=F32)
            out_t = out_t * inverse
            out[:, columns] = out_t.T.astype(BF16)
            grad_t = grad[:, columns].astype(F32).T
            factor = inverse * scale
            delta = jnp.sum(grad_t * out_t, axis=0, keepdims=True) * factor
            grad_t = grad_t * factor
            grad_s = grad_t.T.astype(BF16)
            grad_t = grad_t.astype(BF16)
            yield
            for k in range(span):
                at = slice(k * rows, (k + 1) * rows)
                dp = lax.dot_general(kv[g, k, 1], grad_t, NN, preferred_element_type=F32)
                ds[at, :] = (sc[at, :] * (dp - delta)).astype(BF16)
            acc[g, 1] += lax.dot_general(pr[...], grad_s, NN, preferred_element_type=F32)
            yield
            acc[g, 0] += lax.dot_general(ds[...], q, NN, preferred_element_type=F32)
            dq = lax.dot_general(key_t[...], ds[...], NN, preferred_element_type=F32)
            query_grad[:, columns] = dq.T.astype(BF16)
            yield

        def head(i, _):
            if kv_count > 1:
                @pl.when((i == min(1, steps - 1)) & (g >= 1))
                def _():
                    combine(g - 1)

                @pl.when((i == steps - 1) & (g + 1 < kv_count))
                def _():
                    pass_on(g + 1)
            runs = [one(lead * i + slot, slot) for slot in range(lead)]
            for _ in range(4):
                for run in runs:
                    next(run)
            return 0

        lax.fori_loop(0, steps, head, 0)
        share_partial(g)
        return 0

    lax.fori_loop(0, kv_count, group, 0)
    combine(kv_count - 1)

    def finish(g, _):
        columns = pl.ds(pl.multiple_of(g * ATT_DIM, ATT_DIM), ATT_DIM)

        @pl.when(odd == 0)
        def _():
            wait_mix(g, 0)
            acc[g, 0, 0:rows, :] += mix[g, 0, 0].astype(F32)
            acc[g, 1, 0:rows, :] += mix[g, 0, 1].astype(F32) * scale

        for j in range(1, far + 1):
            @pl.when(me + 2 * j < n)
            def _():
                back(g, j).wait_recv()
                acc[g, 0, 0:rows, :] += got[g, j, 0].astype(F32)
                acc[g, 1, 0:rows, :] += got[g, j, 1].astype(F32) * scale
        dk, dv = partial(g, 0)
        key_grad[:, columns] = dk.astype(BF16)
        value_grad[:, columns] = dv.astype(BF16)
        for j in range(1, far + 1):
            @pl.when(me + 2 * j < n)
            def _():
                gather(g, j).wait_send()

            @pl.when(me - 2 * j >= 0)
            def _():
                back(g, j).wait_send()
        each_hand_on(0, far, lambda j, slot: hand_on(g, j, slot).wait_send())
        each_to_pair(lambda k, j: to_pair(g, k, j).wait_send())
        return 0

    lax.fori_loop(0, kv_count, finish, 0)


def on_device(lengths, query, keys, values, attention_grad):
    n = lax.axis_size("seq")
    rows = query.shape[0]
    kv_count = keys.shape[1] // ATT_DIM
    share = query.shape[1] // keys.shape[1]
    span = n // 2 + 1
    lead = 4
    whole = pl.BlockSpec(memory_space=pltpu.VMEM)
    block = (2, rows, ATT_DIM)
    return pl.pallas_call(
        functools.partial(kernel, n, span, kv_count, share, lead),
        out_shape=[
            jax.ShapeDtypeStruct(a.shape, BF16) for a in (query, query, keys, values)
        ],
        in_specs=[pl.BlockSpec(memory_space=pltpu.SMEM)]
        + [pl.BlockSpec(memory_space=pl.ANY)] * 4,
        out_specs=[whole] * 4,
        scratch_shapes=[
            pltpu.VMEM(query.shape, BF16),
            pltpu.VMEM(query.shape, BF16),
            pltpu.VMEM((kv_count, span) + block, BF16),
            pltpu.VMEM((ATT_DIM, span * rows), BF16),
            pltpu.VMEM((ATT_DIM, span * rows), BF16),
            pltpu.VMEM((lead, span * rows, rows), F32),
            pltpu.VMEM((lead, span * rows, rows), BF16),
            pltpu.VMEM((lead, span * rows, rows), BF16),
            pltpu.VMEM((kv_count, 2, span * rows, ATT_DIM), F32),
            pltpu.VMEM((kv_count, span) + block, BF16),
            pltpu.VMEM((kv_count, span // 2 + 1) + block, BF16),
            pltpu.VMEM((kv_count, span // 2 + 1) + block, BF16),
            pltpu.SemaphoreType.DMA((2 + 2 * kv_count,)),
            pltpu.SemaphoreType.DMA((kv_count, span)),
            pltpu.SemaphoreType.DMA((kv_count, span)),
            pltpu.SemaphoreType.DMA((kv_count, span)),
            pltpu.SemaphoreType.DMA((kv_count, span // 2 + 1)),
            pltpu.SemaphoreType.DMA((kv_count, span // 2 + 1)),
        ],
        compiler_params=pltpu.CompilerParams(
            collective_id=0, has_side_effects=True, vmem_limit_bytes=60 << 20
        ),
    )(lengths, query, keys, values, attention_grad)


def solution(mesh):
    in_specs = (P(), P("seq", "head"), P("seq", "head"), P("seq", "head"), P("seq", "head"))
    out_specs = (P("seq", "head"), P("seq", "head"), P("seq", "head"), P("seq", "head"))
    return jax.shard_map(
        on_device, mesh=mesh, in_specs=in_specs, out_specs=out_specs, check_vma=False
    )
```

```python
import functools

import jax
import jax.numpy as jnp
from jax import lax
from jax.experimental import pallas as pl
from jax.experimental.pallas import tpu as pltpu
from jax.sharding import PartitionSpec as P

ATT_DIM = 128
LOG2E = 1.4426950408889634
MASKED = -1.0e30
MESH = pl.DeviceIdType.MESH

F32 = jnp.float32
BF16 = jnp.bfloat16
NT = (((1,), (1,)), ((), ()))
NN = (((1,), (0,)), ((), ()))


def kernel(
    n, span, kv_count, share, lead,
    lengths, query_hbm, keys, values, grad_hbm,
    out, query_grad, key_grad, value_grad,
    query, grad, kv, key_t, value_t, score, prob, dscore, acc, sent, mix, got,
    load, gather_send, gather_recv, back_send, mix_recv, back_recv,
):
    rows = query.shape[0]
    scale = ATT_DIM ** -0.5
    me = lax.axis_index("seq")
    odd = lax.rem(me, 2)
    pair = me + 1 - 2 * odd
    far = span // 2

    def load_kv(g, which):
        columns = pl.ds(pl.multiple_of(g * ATT_DIM, ATT_DIM), ATT_DIM)
        source = (keys, values)[which]
        return pltpu.make_async_copy(
            source.at[:, columns], kv.at[g, 0, which], load.at[2 + 2 * g + which]
        )

    def start_load(g, _):
        load_kv(g, 0).start()
        load_kv(g, 1).start()
        return 0

    lax.fori_loop(0, kv_count, start_load, 0)
    load_query = pltpu.make_async_copy(query_hbm, query, load.at[0])
    load_grad = pltpu.make_async_copy(grad_hbm, grad, load.at[1])
    load_query.start()
    load_grad.start()

    def signal(barrier, target):
        pl.semaphore_signal(barrier, inc=1, device_id={"seq": target}, device_id_type=MESH)

    barrier = pltpu.get_barrier_semaphore()
    signal(barrier, pair)
    for j in range(1, far + 1):
        @pl.when(me + 2 * j < n)
        def _():
            signal(barrier, me + 2 * j)

        @pl.when(me - 2 * j >= 0)
        def _():
            signal(barrier, me - 2 * j)

    def clear(g, _):
        for k in range(1, span):
            @pl.when(me - k < 0)
            def _():
                kv[g, k] = jnp.zeros((2, rows, ATT_DIM), BF16)
        return 0

    lax.fori_loop(0, kv_count, clear, 0)
    pl.semaphore_wait(
        barrier, 1 + jnp.minimum(me // 2, far) + jnp.minimum((n - 1 - me) // 2, far)
    )

    def remote(source, target, send_sem, recv_sem, device):
        return pltpu.make_async_remote_copy(
            src_ref=source, dst_ref=target, send_sem=send_sem, recv_sem=recv_sem,
            device_id={"seq": device}, device_id_type=MESH,
        )

    def gather(g, j):
        return remote(
            kv.at[g, 0], kv.at[g, 2 * j], gather_send.at[g, 2 * j],
            gather_recv.at[g, 2 * j], me + 2 * j,
        )

    def hand_on(g, j, slot):
        return remote(
            kv.at[g, 2 * j], kv.at[g, slot], gather_send.at[g, slot],
            gather_recv.at[g, slot], pair,
        )

    def each_hand_on(first, last, act):
        for j in range(first, last + 1):
            if j >= 1:
                @pl.when((odd == 1) & (me - 2 * j >= 0))
                def _():
                    act(j, 2 * j - 1)
            if j < far:
                @pl.when((odd == 0) & (me - 2 * j >= 0))
                def _():
                    act(j, 2 * j + 1)

    def begin(g):
        load_kv(g, 0).wait()
        load_kv(g, 1).wait()
        for j in range(1, far + 1):
            @pl.when(me + 2 * j < n)
            def _():
                gather(g, j).start()
        each_hand_on(0, 0, lambda j, slot: hand_on(g, j, slot).start())

    begin(0)

    def pass_on(g):
        for j in range(1, far + 1):
            @pl.when(me - 2 * j >= 0)
            def _():
                gather(g, j).wait_recv()
            each_hand_on(j, j, lambda j, slot: hand_on(g, j, slot).start())

    def partial(g, k):
        at = slice(k * rows, (k + 1) * rows)
        return acc[g, 0, at, :], acc[g, 1, at, :] * (1.0 / scale)

    def to_pair(g, k, j):
        return remote(
            sent.at[g, k], mix.at[g, j], back_send.at[g, k], mix_recv.at[g, j], pair
        )

    def back(g, j):
        return remote(
            sent.at[g, 2 * j], got.at[g, j], back_send.at[g, 2 * j],
            back_recv.at[g, j], me - 2 * j,
        )

    def each_to_pair(act):
        for k in range(span - 2, 0, -2):
            @pl.when((odd == 1) & (me - k >= 0))
            def _():
                act(k, (k - 1) // 2)

            @pl.when((odd == 0) & (me - k >= 0))
            def _():
                act(k, (k + 1) // 2)

    def share_partial(g):
        def act(k, j):
            dk, dv = partial(g, k)
            sent[g, k, 0] = dk.astype(BF16)
            sent[g, k, 1] = dv.astype(BF16)
            to_pair(g, k, j).start()

        each_to_pair(act)

    def wait_mix(g, j):
        to_pair(g, 1, j).wait_recv()

    def combine(g):
        for j in range(far, 0, -1):
            def relay(mixed):
                dk, dv = partial(g, 2 * j)
                if mixed:
                    wait_mix(g, j)
                    dk = dk + mix[g, j, 0].astype(F32)
                    dv = dv + mix[g, j, 1].astype(F32)
                sent[g, 2 * j, 0] = dk.astype(BF16)
                sent[g, 2 * j, 1] = dv.astype(BF16)
                back(g, j).start()

            if j < far:
                @pl.when(me - 2 * j >= 0)
                def _():
                    relay(True)
            else:
                @pl.when((me - 2 * j >= 0) & (odd == 1))
                def _():
                    relay(True)

                @pl.when((me - 2 * j >= 0) & (odd == 0))
                def _():
                    relay(False)

    q_lane = lax.broadcasted_iota(jnp.int32, (1, rows), 1)
    position = q_lane + me * rows
    start = jnp.zeros((1, rows), jnp.int32)
    end = 0
    for i in range(lengths.shape[0]):
        end = end + lengths[i]
        start = jnp.where(position >= end, end, start)

    load_query.wait()
    load_grad.wait()
    pass_on(0)
    steps = share // lead

    def group(g, _):
        for k in range(1, span, 2):
            @pl.when(me - k >= 0)
            def _():
                hand_on(g, 0, k).wait_recv()
        for k in range(span):
            key_t[:, k * rows:(k + 1) * rows] = kv[g, k, 0].T
            value_t[:, k * rows:(k + 1) * rows] = kv[g, k, 1].T
        acc[g] = jnp.zeros(acc.shape[1:], F32)
        if kv_count > 1:
            @pl.when(g + 1 < kv_count)
            def _():
                begin(g + 1)

        def one(i, slot):
            sc, pr, ds = score.at[slot], prob.at[slot], dscore.at[slot]
            columns = pl.ds(pl.multiple_of((g * share + i) * ATT_DIM, ATT_DIM), ATT_DIM)
            q = query[:, columns]
            top = jnp.full((1, rows), MASKED, F32)
            k_row = lax.broadcasted_iota(jnp.int32, (rows, rows), 0)
            for k in range(span):
                s = lax.dot_general(kv[g, k, 0], q, NT, preferred_element_type=F32)
                allow = k_row >= start - (me - k) * rows
                if k == 0:
                    allow = allow & (k_row <= q_lane)
                s = jnp.where(allow, s, MASKED)
                sc[k * rows:(k + 1) * rows, :] = s
                top = jnp.maximum(top, jnp.max(s, axis=0, keepdims=True))
            yield
            mass = jnp.zeros((1, rows), F32)
            for k in range(span):
                at = slice(k * rows, (k + 1) * rows)
                p = jnp.exp2((sc[at, :] - top) * (scale * LOG2E))
                mass = mass + jnp.sum(p, axis=0, keepdims=True)
                sc[at, :] = p
                pr[at, :] = p.astype(BF16)
            inverse = 1.0 / mass
            out_t = lax.dot_general(value_t[...], pr[...], NN, preferred_element_type=F32)
            out_t = out_t * inverse
            out[:, columns] = out_t.T.astype(BF16)
            grad_t = grad[:, columns].astype(F32).T
            factor = inverse * scale
            delta = jnp.sum(grad_t * out_t, axis=0, keepdims=True) * factor
            grad_t = grad_t * factor
            grad_s = grad_t.T.astype(BF16)
            grad_t = grad_t.astype(BF16)
            yield
            for k in range(span):
                at = slice(k * rows, (k + 1) * rows)
                dp = lax.dot_general(kv[g, k, 1], grad_t, NN, preferred_element_type=F32)
                ds[at, :] = (sc[at, :] * (dp - delta)).astype(BF16)
            acc[g, 1] += lax.dot_general(pr[...], grad_s, NN, preferred_element_type=F32)
            yield
            acc[g, 0] += lax.dot_general(ds[...], q, NN, preferred_element_type=F32)
            dq = lax.dot_general(key_t[...], ds[...], NN, preferred_element_type=F32)
            query_grad[:, columns] = dq.T.astype(BF16)
            yield

        def head(i, _):
            if kv_count > 1:
                @pl.when((i == min(1, steps - 1)) & (g >= 1))
                def _():
                    combine(g - 1)

                @pl.when((i == steps - 1) & (g + 1 < kv_count))
                def _():
                    pass_on(g + 1)
            runs = [one(lead * i + slot, slot) for slot in range(lead)]
            for _ in range(4):
                for run in runs:
                    next(run)
            return 0

        lax.fori_loop(0, steps, head, 0)
        share_partial(g)
        return 0

    lax.fori_loop(0, kv_count, group, 0)
    combine(kv_count - 1)

    def finish(g, _):
        columns = pl.ds(pl.multiple_of(g * ATT_DIM, ATT_DIM), ATT_DIM)

        @pl.when(odd == 0)
        def _():
            wait_mix(g, 0)
            acc[g, 0, 0:rows, :] += mix[g, 0, 0].astype(F32)
            acc[g, 1, 0:rows, :] += mix[g, 0, 1].astype(F32) * scale

        for j in range(1, far + 1):
            @pl.when(me + 2 * j < n)
            def _():
                back(g, j).wait_recv()
                acc[g, 0, 0:rows, :] += got[g, j, 0].astype(F32)
                acc[g, 1, 0:rows, :] += got[g, j, 1].astype(F32) * scale
        dk, dv = partial(g, 0)
        key_grad[:, columns] = dk.astype(BF16)
        value_grad[:, columns] = dv.astype(BF16)
        for j in range(1, far + 1):
            @pl.when(me + 2 * j < n)
            def _():
                gather(g, j).wait_send()

            @pl.when(me - 2 * j >= 0)
            def _():
                back(g, j).wait_send()
        each_hand_on(0, far, lambda j, slot: hand_on(g, j, slot).wait_send())
        each_to_pair(lambda k, j: to_pair(g, k, j).wait_send())
        return 0

    lax.fori_loop(0, kv_count, finish, 0)


def on_device(lengths, query, keys, values, attention_grad):
    n = lax.axis_size("seq")
    rows = query.shape[0]
    kv_count = keys.shape[1] // ATT_DIM
    share = query.shape[1] // keys.shape[1]
    span = n // 2 + 1
    lead = 4
    whole = pl.BlockSpec(memory_space=pltpu.VMEM)
    block = (2, rows, ATT_DIM)
    return pl.pallas_call(
        functools.partial(kernel, n, span, kv_count, share, lead),
        out_shape=[
            jax.ShapeDtypeStruct(a.shape, BF16) for a in (query, query, keys, values)
        ],
        in_specs=[pl.BlockSpec(memory_space=pltpu.SMEM)]
        + [pl.BlockSpec(memory_space=pl.ANY)] * 4,
        out_specs=[whole] * 4,
        scratch_shapes=[
            pltpu.VMEM(query.shape, BF16),
            pltpu.VMEM(query.shape, BF16),
            pltpu.VMEM((kv_count, span) + block, BF16),
            pltpu.VMEM((ATT_DIM, span * rows), BF16),
            pltpu.VMEM((ATT_DIM, span * rows), BF16),
            pltpu.VMEM((lead, span * rows, rows), F32),
            pltpu.VMEM((lead, span * rows, rows), BF16),
            pltpu.VMEM((lead, span * rows, rows), BF16),
            pltpu.VMEM((kv_count, 2, span * rows, ATT_DIM), F32),
            pltpu.VMEM((kv_count, span) + block, BF16),
            pltpu.VMEM((kv_count, span // 2 + 1) + block, BF16),
            pltpu.VMEM((kv_count, span // 2 + 1) + block, BF16),
            pltpu.SemaphoreType.DMA((2 + 2 * kv_count,)),
            pltpu.SemaphoreType.DMA((kv_count, span)),
            pltpu.SemaphoreType.DMA((kv_count, span)),
            pltpu.SemaphoreType.DMA((kv_count, span)),
            pltpu.SemaphoreType.DMA((kv_count, span // 2 + 1)),
            pltpu.SemaphoreType.DMA((kv_count, span // 2 + 1)),
        ],
        compiler_params=pltpu.CompilerParams(
            collective_id=0, has_side_effects=True, vmem_limit_bytes=60 << 20
        ),
    )(lengths, query, keys, values, attention_grad)


def solution(mesh):
    in_specs = (P(), P("seq", "head"), P("seq", "head"), P("seq", "head"), P("seq", "head"))
    out_specs = (P("seq", "head"), P("seq", "head"), P("seq", "head"), P("seq", "head"))
    return jax.shard_map(
        on_device, mesh=mesh, in_specs=in_specs, out_specs=out_specs, check_vma=False
    )
```
